512 devices in a mesh: ta: 8 (over z), gx: 64 (over x, y, core).
Axes of the slice: x: 4, y: 8, z: 8, core: 2. Of those that a mesh axis runs over, the one named last changes fastest.
Arguments:
- gauge_links: float32 [3, 2, 3, 3, 512, 9216], P(None, None, None, None, ('ta', 'gx')), parts along dimension 4, may hold values from -1 to 1, as said below
Outputs:
- fixed_links: float32 [3, 2, 3, 3, 512, 9216], P(None, None, None, None, ('ta', 'gx')), parts along dimension 4
- drift_values: float32 [8], P('ta'), parts along dimension 0
The draws below stay inside these ranges and needn't reach their ends.
There are 8 independent parts, one for each index of `ta`. The reference program is written for one: setup_inputs(seed, part) draws one part's arguments, and reference() takes and returns one part's arrays. A program takes and returns all parts, laid end to end along the dimension named above; each array names one. Nothing has to cross between parts.
Inputs may be any that keep to these rules, and one draw needn't show every extreme that they name: `gauge_links`: for every direction and site the complex matrix is unitary.
All inputs are finite; a program needn't handle non-finite values.
Results may differ from the reference program's by a relative error of at most 0.0003.
Values sent between devices are 32-bit elements; how exact they have to be, the bound alone decides.
A program may use at most 128 MiB of HBM per device.

```python
import math
import jax
import jax.numpy as jnp

SIDE = 96
ITERS = 1
NX = 64


def matrix_mul_drawn(left, right):
    return jnp.sum(left[:, :, None] * right[None, :, :], axis=1)


def complex_mul_drawn(left, right):
    real_part = matrix_mul_drawn(left[0], right[0]) - matrix_mul_drawn(left[1], right[1])
    imag_part = matrix_mul_drawn(left[0], right[1]) + matrix_mul_drawn(left[1], right[0])
    return (real_part, imag_part)


def scalar_mul_drawn(left, right):
    return (left[0] * right[0] - left[1] * right[1], left[0] * right[1] + left[1] * right[0])


def inverse_three_drawn(real_part, imag_part):

    def entry(i, j):
        return (real_part[i % 3, j % 3], imag_part[i % 3, j % 3])
    cofactor = []
    for i in range(3):
        row_list = []
        for j in range(3):
            first = scalar_mul_drawn(entry(i + 1, j + 1), entry(i + 2, j + 2))
            second = scalar_mul_drawn(entry(i + 1, j + 2), entry(i + 2, j + 1))
            row_list.append((first[0] - second[0], first[1] - second[1]))
        cofactor.append(row_list)
    det_real = 0.0
    det_imag = 0.0
    for j in range(3):
        term = scalar_mul_drawn(entry(0, j), cofactor[0][j])
        det_real = det_real + term[0]
        det_imag = det_imag + term[1]
    denom = det_real * det_real + det_imag * det_imag
    recip = (det_real / denom, -det_imag / denom)
    rows_real = []
    rows_imag = []
    for i in range(3):
        line_real = []
        line_imag = []
        for j in range(3):
            value = scalar_mul_drawn(cofactor[j][i], recip)
            line_real.append(value[0])
            line_imag.append(value[1])
        rows_real.append(jnp.stack(line_real))
        rows_imag.append(jnp.stack(line_imag))
    return (jnp.stack(rows_real), jnp.stack(rows_imag))


def make_unitary(fields):
    empty_part = jnp.zeros_like(fields[0])
    rows_real = [[empty_part, fields[2], fields[4]], [-fields[2], empty_part, fields[6]], [-fields[4], -fields[6], empty_part]]
    rows_imag = [[fields[0], fields[3], fields[5]], [fields[3], fields[1], fields[7]], [fields[5], fields[7], -(fields[0] + fields[1])]]
    gen_real = jnp.stack([jnp.stack(r) for r in rows_real])
    gen_imag = jnp.stack([jnp.stack(r) for r in rows_imag])
    eye_full = jnp.eye(3, dtype=jnp.float32).reshape((3, 3) + (1,) * (gen_real.ndim - 2))
    lower = inverse_three_drawn(eye_full - 0.5 * gen_real, -0.5 * gen_imag)
    upper = (eye_full + 0.5 * gen_real, 0.5 * gen_imag)
    return jnp.stack(complex_mul_drawn(upper, lower))


def draw_gauge_links(key, part):
    coord_x = jnp.arange(NX, dtype=jnp.float32) / (NX - 1)
    coord_s = jnp.arange(SIDE, dtype=jnp.float32) / (SIDE - 1)
    shape = (3, 8, NX, SIDE, SIDE)
    noise = jax.random.normal(key, shape, jnp.float32)
    scale = 0.15 * jnp.power(10.0, 0.5 * coord_x[:, None, None] + 0.5 * coord_s[None, :, None])
    fields = noise * scale
    built = jnp.stack([make_unitary(fields[d]) for d in range(3)])
    return built.reshape(3, 2, 3, 3, NX, SIDE * SIDE).astype(jnp.float32)


def setup_inputs(seed: int = 0, part: int = 0) -> dict:
    splits = jax.random.split(jax.random.key(seed), 2)
    part_splits = jax.random.split(jax.random.fold_in(splits[1], part), 2)
    return {
        "gauge_links": draw_gauge_links(jax.random.fold_in(jax.random.fold_in(splits[1], part), 71), part),
    }


step_size = 0.08
peak_square = 12.0


def matrix_mul(left, right):
    return jnp.sum(left[:, :, None] * right[None, :, :], axis=1)


def complex_mul(left, right):
    real_part = matrix_mul(left[0], right[0]) - matrix_mul(left[1], right[1])
    imag_part = matrix_mul(left[0], right[1]) + matrix_mul(left[1], right[0])
    return real_part, imag_part


def dagger(matrix):
    return jnp.swapaxes(matrix[0], 0, 1), -jnp.swapaxes(matrix[1], 0, 1)


def scalar_mul(left, right):
    return left[0] * right[0] - left[1] * right[1], left[0] * right[1] + left[1] * right[0]


def inverse_three(real_part, imag_part):
    def entry(i, j):
        return real_part[i % 3, j % 3], imag_part[i % 3, j % 3]

    cofactor = []
    for i in range(3):
        row_list = []
        for j in range(3):
            first = scalar_mul(entry(i + 1, j + 1), entry(i + 2, j + 2))
            second = scalar_mul(entry(i + 1, j + 2), entry(i + 2, j + 1))
            row_list.append((first[0] - second[0], first[1] - second[1]))
        cofactor.append(row_list)
    det_real = 0.0
    det_imag = 0.0
    for j in range(3):
        term = scalar_mul(entry(0, j), cofactor[0][j])
        det_real = det_real + term[0]
        det_imag = det_imag + term[1]
    denom = det_real * det_real + det_imag * det_imag
    recip = (det_real / denom, -det_imag / denom)
    rows_real = []
    rows_imag = []
    for i in range(3):
        line_real = []
        line_imag = []
        for j in range(3):
            value = scalar_mul(cofactor[j][i], recip)
            line_real.append(value[0])
            line_imag.append(value[1])
        rows_real.append(jnp.stack(line_real))
        rows_imag.append(jnp.stack(line_imag))
    return jnp.stack(rows_real), jnp.stack(rows_imag)


def identity_like(array):
    return jnp.eye(3, dtype=jnp.float32).reshape((3, 3) + (1,) * (array.ndim - 2))


def cayley(matrix):
    eye_full = identity_like(matrix[0])
    lower_real, lower_imag = inverse_three(eye_full - 0.5 * matrix[0], -0.5 * matrix[1])
    upper = (eye_full + 0.5 * matrix[0], 0.5 * matrix[1])
    return complex_mul(upper, (lower_real, lower_imag))


def rebuild(fields):
    empty_part = jnp.zeros_like(fields[0])
    rows_real = [[empty_part, fields[2], fields[4]], [-fields[2], empty_part, fields[6]], [-fields[4], -fields[6], empty_part]]
    rows_imag = [[fields[0], fields[3], fields[5]], [fields[3], fields[1], fields[7]], [fields[5], fields[7], -(fields[0] + fields[1])]]
    return jnp.stack([jnp.stack(r) for r in rows_real]), jnp.stack([jnp.stack(r) for r in rows_imag])


def traceless(div_real, div_imag):
    anti_real = 0.5 * (div_real - jnp.swapaxes(div_real, 0, 1))
    anti_imag = 0.5 * (div_imag + jnp.swapaxes(div_imag, 0, 1))
    trace_part = (anti_imag[0, 0] + anti_imag[1, 1] + anti_imag[2, 2]) / 3.0
    anti_imag = anti_imag - identity_like(anti_imag) * trace_part
    fields = jnp.stack([anti_imag[0, 0], anti_imag[1, 1], anti_real[0, 1], anti_imag[0, 1], anti_real[0, 2], anti_imag[0, 2], anti_real[1, 2], anti_imag[1, 2]])
    return anti_real, anti_imag, fields


def sine_square(index, length):
    value = jnp.sin(index.astype(jnp.float32) * (math.pi / length))
    return 4.0 * value * value


def reference(gauge_links):
    count_x = gauge_links.shape[4]
    cells = SIDE * SIDE
    merged = jnp.arange(cells, dtype=jnp.int32)
    square_x = sine_square(jnp.arange(count_x, dtype=jnp.int32), count_x)
    square_yz = sine_square(merged // SIDE, SIDE) + sine_square(merged % SIDE, SIDE)
    total = square_x[:, None] + square_yz[None, :]
    safe = jnp.where(total > 0, total, 1.0)
    kernel = jnp.where(total > 0, peak_square / safe, 0.0).reshape(count_x, SIDE, SIDE)
    state = gauge_links
    values = []
    for turn in range(ITERS):
        cube = state.reshape(3, 2, 3, 3, count_x, SIDE, SIDE)
        diverge = jnp.roll(cube[0], 1, axis=3) - cube[0]
        diverge = diverge + jnp.roll(cube[1], 1, axis=4) - cube[1]
        diverge = diverge + jnp.roll(cube[2], 1, axis=5) - cube[2]
        anti_real, anti_imag, fields = traceless(diverge[0], diverge[1])
        values.append(jnp.sum(anti_real * anti_real + anti_imag * anti_imag) / (9.0 * count_x * cells))
        spectrum = jnp.fft.fftn(fields, axes=(1, 2, 3)) * kernel
        filtered = jnp.real(jnp.fft.ifftn(spectrum, axes=(1, 2, 3))).astype(jnp.float32)
        rotation = cayley(rebuild(step_size * filtered))
        updated = []
        for d in range(3):
            ahead = (jnp.roll(rotation[0], -1, axis=2 + d), jnp.roll(rotation[1], -1, axis=2 + d))
            moved = complex_mul(complex_mul(rotation, (cube[d, 0], cube[d, 1])), dagger(ahead))
            updated.append(jnp.stack(moved))
        state = jnp.stack(updated).reshape(3, 2, 3, 3, count_x, cells)
    return state, jnp.stack(values)
```

```python
import math

import jax
import jax.numpy as jnp
import numpy as np
from jax import lax
from jax.experimental import pallas as pl
from jax.experimental.pallas import tpu as pltpu
from jax.sharding import PartitionSpec as P

SIDE = 96
NX = 64
CELLS = SIDE * SIDE
ROWS, LANES = 24, 384
STEP_SIZE = 0.08
PEAK_SQUARE = 12.0
MESH = pl.DeviceIdType.MESH
F32 = jnp.float32
BF16 = jnp.bfloat16


def cas(length):
    index = np.arange(length)
    angle = 2.0 * np.pi * ((index[:, None] * index[None, :]) % length) / length
    return np.cos(angle) + np.sin(angle)


def sine_square(length):
    return 4.0 * np.sin(np.pi * np.arange(length) / length) ** 2


def halves(table):
    table = np.asarray(table, np.float32)
    high = table.astype(BF16)
    low = (table - high.astype(np.float32)).astype(BF16)
    return np.stack([high, low])


def make_tables():
    side = cas(SIDE)
    spread = np.zeros((LANES, 512))
    for k in range(4):
        spread[96 * k : 96 * k + 96, 128 * k : 128 * k + 96] = side
    order = np.array([4 * h + k for k in range(4) for h in range(ROWS)])
    down = side[:, order]
    square = sine_square(SIDE)
    plane = np.zeros((NX, 9, 128), np.float32)
    lane = np.arange(128)
    for owner in range(NX):
        for i in range(9):
            tile = 9 * (owner // 8) + i
            row = (tile // 6) * 8 + owner % 8
            part = tile % 3
            column = np.where(lane < 96, lane, 32 * part + lane - 96)
            plane[owner, i] = square[row] + square[column]
    along = np.broadcast_to(sine_square(NX)[:, None], (NX, 128)).astype(np.float32)
    return (
        halves(spread),
        halves(spread.T),
        halves(down),
        halves(down.T),
        halves(cas(NX)),
        plane,
        np.ascontiguousarray(along),
    )


def split(x):
    high = x.astype(BF16)
    return high, (x - high.astype(F32)).astype(BF16)


def dot(a, b):
    return jnp.dot(a, b, preferred_element_type=F32)


def data_times(x, table):
    high, low = split(x)
    return dot(high, table[0]) + (dot(low, table[0]) + dot(high, table[1]))


def times_data(table, x):
    high, low = split(x)
    return dot(table[0], high) + (dot(table[0], low) + dot(table[1], high))


def projected(get):
    im0, im1, im2 = get(1, 0, 0), get(1, 1, 1), get(1, 2, 2)
    third = (im0 + im1 + im2) * (1.0 / 3.0)
    out = [im0 - third, im1 - third]
    for i, j in ((0, 1), (0, 2), (1, 2)):
        out.append(0.5 * (get(0, i, j) - get(0, j, i)))
        out.append(0.5 * (get(1, i, j) + get(1, j, i)))
    return out


def cayley(a):
    h0, h1, q01, p01, q02, p02, q12, p12 = a
    h2 = -(h0 + h1)
    s01 = p01 * p01 + q01 * q01
    s02 = p02 * p02 + q02 * q02
    s12 = p12 * p12 + q12 * q12
    t0, t1, t2 = h0 * h0, h1 * h1, h2 * h2
    plus = 1.0 + (0.5 * (t0 + t1 + t2) + (s01 + s02 + s12))
    mr = p01 * p12 - q01 * q12
    mi = -(p01 * q12 + q01 * p12)
    nr = p02 * p12 + q02 * q12
    ni = p02 * q12 - q02 * p12
    kr = p01 * p02 + q01 * q02
    ki = q01 * p02 - p01 * q02
    delta = h0 * h1 * h2 + 2.0 * (mr * p02 - mi * q02) - (h0 * s12 + h1 * s02 + h2 * s01)
    scale = 2.0 / (plus * plus + delta * delta)
    u = plus * scale
    v = -delta * scale
    real = [[None] * 3 for _ in range(3)]
    imag = [[None] * 3 for _ in range(3)]
    for i, (h, b) in enumerate(
        (
            (h0, plus - (t0 + s01 + s02)),
            (h1, plus - (t1 + s01 + s12)),
            (h2, plus - (t2 + s02 + s12)),
        )
    ):
        real[i][i] = u * b - v * h - 1.0
        imag[i][i] = u * h + v * b
    for i, j, p, q, br, bi in (
        (0, 1, p01, q01, h2 * p01 - nr, -h2 * q01 - ni),
        (0, 2, p02, q02, h1 * p02 - mr, -h1 * q02 - mi),
        (1, 2, p12, q12, h0 * p12 - kr, -h0 * q12 - ki),
    ):
        ur, ui = br + q, bi + p
        lr, li = br - q, p - bi
        real[i][j] = u * ur - v * ui
        imag[i][j] = u * ui + v * ur
        real[j][i] = u * lr - v * li
        imag[j][i] = u * li + v * lr
    return [real[i][j] for i in range(3) for j in range(3)] + [imag[i][j] for i in range(3) for j in range(3)]


def moved(g, u, ahead):
    tr, ti = [], []
    for i in range(3):
        for j in range(3):
            r = m = None
            for k in range(3):
                ar, ai = g[3 * i + k], g[9 + 3 * i + k]
                br, bi = u[3 * k + j], u[9 + 3 * k + j]
                x, y = ar * br - ai * bi, ar * bi + ai * br
                r, m = (x, y) if r is None else (r + x, m + y)
            tr.append(r)
            ti.append(m)
    out_r, out_i = [], []
    for i in range(3):
        for j in range(3):
            r = m = None
            for k in range(3):
                ar, ai = tr[3 * i + k], ti[3 * i + k]
                br, bi = ahead[3 * j + k], ahead[9 + 3 * j + k]
                x, y = ar * br + ai * bi, ai * br - ar * bi
                r, m = (x, y) if r is None else (r + x, m + y)
            out_r.append(r)
            out_i.append(m)
    return out_r + out_i


def forward_modes(fields, spread, down, tiles_ref):
    part = data_times(fields, spread)
    stacked = jnp.concatenate(
        [
            jnp.concatenate([part[24 * f : 24 * f + 24, 128 * k : 128 * k + 128] for f in range(8)], axis=1)
            for k in range(4)
        ],
        axis=0,
    )
    modes = times_data(down, stacked)
    lane = lax.broadcasted_iota(jnp.int32, (SIDE, 128), 1)
    for q in range(2):
        last = modes[:, 128 * (4 * q + 3) : 128 * (4 * q + 4)]
        for j in range(3):
            own = modes[:, 128 * (4 * q + j) : 128 * (4 * q + j + 1)]
            shift = 96 - 32 * j
            tile = jnp.where(lane < 96, own, pltpu.roll(last, shift, 1))
            for b in range(12):
                tiles_ref[6 * b + 3 * q + j] = tile[8 * b : 8 * b + 8]


def inverse_fields(tiles_ref, spread_t, down_t):
    lane = lax.broadcasted_iota(jnp.int32, (SIDE, 128), 1)
    blocks = []
    for q in range(2):
        tiles = [
            jnp.concatenate([tiles_ref[6 * b + 3 * q + j] for b in range(12)], axis=0) for j in range(3)
        ]
        rolled = [pltpu.roll(tiles[j], 32 * j + 32, 1) for j in range(3)]
        last = jnp.where(lane < 32, rolled[0], jnp.where(lane < 64, rolled[1], rolled[2]))
        blocks += tiles + [last]
    stacked = times_data(down_t, jnp.concatenate(blocks, axis=1))
    part = jnp.concatenate(
        [
            jnp.concatenate([stacked[24 * k : 24 * k + 24, 128 * f : 128 * f + 128] for k in range(4)], axis=1)
            for f in range(8)
        ],
        axis=0,
    )
    return data_times(part, spread_t)


def row_turned(x, shift):
    count = x.shape[0] // ROWS
    return pltpu.roll(x.reshape(count, ROWS, x.shape[1]), shift, 1).reshape(x.shape)


def lane_of(x):
    return lax.broadcasted_iota(jnp.int32, x.shape, 1)


def from_y_before(x):
    turned = pltpu.roll(x, 96, 1)
    return jnp.where(lane_of(x) < 96, row_turned(turned, 1), turned)


def from_z_before(x):
    return jnp.where(lane_of(x) % 96 == 0, pltpu.roll(x, LANES - 95, 1), pltpu.roll(x, 1, 1))


def from_y_after(x):
    turned = pltpu.roll(x, LANES - 96, 1)
    return jnp.where(lane_of(x) >= 288, row_turned(turned, ROWS - 1), turned)


def from_z_after(x):
    return jnp.where(lane_of(x) % 96 == 95, pltpu.roll(x, 95, 1), pltpu.roll(x, LANES - 1, 1))


def kernel(
    u_hbm, spread_hbm, spread_t_hbm, down, down_t, along, plane_hbm, square_x,
    out_hbm, drift_ref,
    u, spread, spread_t, plane, own, prev, rest, snd, rcv, sol, back, ahead, part, parts,
    g, gy, gz, gx, act,
    local_sem, edge_sem, out_send, out_recv, back_send, back_recv, part_send, part_recv,
):
    me = lax.axis_index("gx")
    after, before = lax.rem(me + 1, NX), lax.rem(me + NX - 1, NX)

    loads = [
        pltpu.make_async_copy(u_hbm.at[pl.ds(18 * d, 18)], u.at[pl.ds(18 * d, 18)], local_sem.at[d])
        for d in range(3)
    ]
    loads.append(pltpu.make_async_copy(spread_hbm, spread, local_sem.at[3]))
    loads.append(pltpu.make_async_copy(spread_t_hbm, spread_t, local_sem.at[4]))
    loads.append(pltpu.make_async_copy(plane_hbm.at[me], plane, local_sem.at[5]))
    for load in loads:
        load.start()

    barrier = pltpu.get_barrier_semaphore()

    def greet(k, carry):
        peer = lax.rem(me + k, NX)
        pl.semaphore_signal(barrier, inc=1, device_id={"gx": peer}, device_id_type=MESH)
        return carry

    lax.fori_loop(1, NX, greet, 0)

    def project(d, into):
        for j in range(3):
            fields = projected(
                lambda p, a, b: u[18 * d + 9 * p + 3 * a + b, pl.ds(j, ROWS, stride=3), :]
            )
            for f in range(8):
                into[pl.ds(ROWS * f, ROWS), pl.ds(128 * j, 128)] = fields[f]

    loads[0].wait()
    project(0, own)
    pl.semaphore_wait(barrier, NX - 1)

    edge = pltpu.make_async_remote_copy(
        src_ref=own, dst_ref=prev, send_sem=edge_sem.at[0], recv_sem=edge_sem.at[1],
        device_id={"gx": after}, device_id_type=MESH,
    )
    edge.start()

    loads[1].wait()
    project(1, act)
    middle = act[...]
    rest[...] = from_y_before(middle) - middle - own[...]
    loads[2].wait()
    project(2, act)
    middle = act[...]
    rest[...] += from_z_before(middle) - middle
    loads[3].wait()
    loads[4].wait()
    loads[5].wait()

    edge.wait()
    fields = rest[...] + prev[...]
    f0, f1, tail = fields[:24], fields[24:48], fields[48:]
    both = f0 + f1
    square = f0 * f0 + f1 * f1 + both * both
    total = jnp.sum(square, axis=0, keepdims=True) + 2.0 * jnp.sum(tail * tail, axis=0, keepdims=True)
    total = total[:, :128] + total[:, 128:256] + total[:, 256:]
    part[...] = jnp.broadcast_to(total, (8, 128))
    forward_modes(fields, spread, down, snd)

    group, line = me // 8, lax.rem(me, 8)

    def there(peer):
        return pltpu.make_async_remote_copy(
            src_ref=snd.at[pl.ds(9 * (peer // 8), 9), lax.rem(peer, 8)], dst_ref=rcv.at[:, me],
            send_sem=out_send.at[peer], recv_sem=out_recv.at[me],
            device_id={"gx": peer}, device_id_type=MESH,
        )

    def there_from(peer):
        return pltpu.make_async_remote_copy(
            src_ref=snd.at[pl.ds(9 * (peer // 8), 9), lax.rem(peer, 8)], dst_ref=rcv.at[:, peer],
            send_sem=out_send.at[peer], recv_sem=out_recv.at[peer],
            device_id={"gx": peer}, device_id_type=MESH,
        )

    def home(peer):
        return pltpu.make_async_remote_copy(
            src_ref=sol.at[:, peer], dst_ref=back.at[pl.ds(9 * group, 9), line],
            send_sem=back_send.at[peer], recv_sem=back_recv.at[me],
            device_id={"gx": peer}, device_id_type=MESH,
        )

    def home_from(peer):
        return pltpu.make_async_remote_copy(
            src_ref=sol.at[:, peer], dst_ref=back.at[pl.ds(9 * (peer // 8), 9), lax.rem(peer, 8)],
            send_sem=back_send.at[peer], recv_sem=back_recv.at[peer],
            device_id={"gx": peer}, device_id_type=MESH,
        )

    def shared(peer):
        return pltpu.make_async_remote_copy(
            src_ref=part.at[0], dst_ref=parts.at[me],
            send_sem=part_send.at[peer], recv_sem=part_recv.at[me],
            device_id={"gx": peer}, device_id_type=MESH,
        )

    def shared_from(peer):
        return pltpu.make_async_remote_copy(
            src_ref=part.at[0], dst_ref=parts.at[peer],
            send_sem=part_send.at[peer], recv_sem=part_recv.at[peer],
            device_id={"gx": peer}, device_id_type=MESH,
        )

    def each(action, sign):
        def body(k, carry):
            action(lax.rem(me + NX + sign * k, NX))
            return carry

        lax.fori_loop(1, NX, body, 0)

    each(lambda peer: there(peer).start(), 1)
    mine = pltpu.make_async_copy(snd.at[pl.ds(9 * group, 9), line], rcv.at[:, me], local_sem.at[0])
    mine.start()
    each(lambda peer: shared(peer).start(), 1)
    own_part = pltpu.make_async_copy(part.at[0], parts.at[me], local_sem.at[1])
    own_part.start()

    factor = PEAK_SQUARE * STEP_SIZE * 0.5 / (NX * CELLS)
    filters = []
    for i in range(9):
        square = square_x[...] + plane[pl.ds(i, 1), :]
        positive = square > 0.0
        filters.append(jnp.where(positive, factor / jnp.where(positive, square, 1.0), 0.0))
    filters = jnp.concatenate(filters, axis=1)

    mine.wait()
    each(lambda peer: there_from(peer).wait(), -1)

    waves = times_data(along, jnp.concatenate([rcv[i] for i in range(9)], axis=1))
    waves = times_data(along, waves * filters)
    for i in range(9):
        sol[i] = waves[:, 128 * i : 128 * i + 128]

    each(lambda peer: home(peer).start(), 1)
    mine = pltpu.make_async_copy(sol.at[:, me], back.at[pl.ds(9 * group, 9), line], local_sem.at[0])
    mine.start()

    own_part.wait()
    each(lambda peer: shared_from(peer).wait(), -1)
    drift_ref[0] = jnp.sum(parts[...]) * (1.0 / (9.0 * NX * CELLS))

    mine.wait()
    each(lambda peer: home_from(peer).wait(), -1)

    onward = pltpu.make_async_remote_copy(
        src_ref=back, dst_ref=ahead, send_sem=edge_sem.at[2], recv_sem=edge_sem.at[3],
        device_id={"gx": before}, device_id_type=MESH,
    )
    onward.start()

    def rotate(tiles, into):
        act[...] = inverse_fields(tiles, spread_t, down_t)

        def body(c, carry):
            r, j = pl.multiple_of(8 * (c // 3), 8), pl.multiple_of(128 * (c % 3), 128)
            entries = cayley([act[pl.ds(ROWS * f + r, 8), pl.ds(j, 128)] for f in range(8)])
            for e in range(18):
                into[pl.ds(ROWS * e + r, 8), pl.ds(j, 128)] = entries[e]
            return carry

        lax.fori_loop(0, 9, body, 0)

    rotate(back, g)
    whole = g[...]
    gy[...] = from_y_after(whole)
    gz[...] = from_z_after(whole)

    stores = []

    def update(d, aheads):
        def body(c, carry):
            i, t = c // 3, c % 3
            r, j = pl.multiple_of(8 * i, 8), pl.multiple_of(128 * t, 128)
            read = lambda ref: [ref[pl.ds(ROWS * e + r, 8), pl.ds(j, 128)] for e in range(18)]
            links = [u[18 * d + e, pl.ds(24 * i + t, 8, stride=3), :] for e in range(18)]
            new = moved(read(g), links, read(aheads))
            for e in range(18):
                u[18 * d + e, pl.ds(24 * i + t, 8, stride=3), :] = new[e]
            return carry

        lax.fori_loop(0, 9, body, 0)
        store = pltpu.make_async_copy(
            u.at[pl.ds(18 * d, 18)], out_hbm.at[pl.ds(18 * d, 18)], local_sem.at[d]
        )
        store.start()
        stores.append(store)

    update(1, gy)
    update(2, gz)
    onward.wait()
    rotate(ahead, gx)
    update(0, gx)
    for store in stores:
        store.wait()


def local(gauge_links):
    tables = make_tables()
    spread, spread_t, down, down_t, along, plane, square_x = (jnp.asarray(t) for t in tables)
    vmem = pl.BlockSpec(memory_space=pltpu.VMEM)
    anywhere = pl.BlockSpec(memory_space=pl.ANY)
    dma = pltpu.SemaphoreType.DMA
    fields = pltpu.VMEM((8 * ROWS, LANES), F32)
    matrix = pltpu.VMEM((18 * ROWS, LANES), F32)
    tiles = pltpu.VMEM((72, 8, 128), F32)
    waves = pltpu.VMEM((9, NX, 128), F32)
    links, drift = pl.pallas_call(
        kernel,
        out_shape=(
            jax.ShapeDtypeStruct((54, 72, 128), F32),
            jax.ShapeDtypeStruct((1,), F32),
        ),
        in_specs=[anywhere, anywhere, anywhere, vmem, vmem, vmem, anywhere, vmem],
        out_specs=(anywhere, pl.BlockSpec(memory_space=pltpu.SMEM)),
        scratch_shapes=[
            pltpu.VMEM((54, 72, 128), F32),
            pltpu.VMEM((2, LANES, 512), BF16),
            pltpu.VMEM((2, 512, LANES), BF16),
            pltpu.VMEM((9, 128), F32),
            fields, fields, fields,
            tiles, waves, waves, tiles, tiles,
            pltpu.VMEM((8, 128), F32),
            pltpu.VMEM((NX, 128), F32),
            matrix, matrix, matrix, matrix,
            fields,
            dma((6,)), dma((4,)),
            dma((NX,)), dma((NX,)), dma((NX,)), dma((NX,)), dma((NX,)), dma((NX,)),
        ],
        compiler_params=pltpu.CompilerParams(collective_id=0, has_side_effects=True),
    )(gauge_links.reshape(54, 72, 128), spread, spread_t, down, down_t, along, plane, square_x)
    return links.reshape(gauge_links.shape), drift


def solution(mesh):
    split_x = ("ta", "gx")
    return jax.shard_map(
        local,
        mesh=mesh,
        in_specs=(P(None, None, None, None, split_x, None),),
        out_specs=(P(None, None, None, None, split_x, None), P("ta")),
        check_vma=False,
    )
```

```python
import math

import jax
import jax.numpy as jnp
import numpy as np
from jax import lax
from jax.experimental import pallas as pl
from jax.experimental.pallas import tpu as pltpu
from jax.sharding import PartitionSpec as P

SIDE = 96
NX = 64
CELLS = SIDE * SIDE
ROWS, LANES = 24, 384
STEP_SIZE = 0.08
PEAK_SQUARE = 12.0
MESH = pl.DeviceIdType.MESH
F32 = jnp.float32
BF16 = jnp.bfloat16


def cas(length):
    index = np.arange(length)
    angle = 2.0 * np.pi * ((index[:, None] * index[None, :]) % length) / length
    return np.cos(angle) + np.sin(angle)


def sine_square(length):
    return 4.0 * np.sin(np.pi * np.arange(length) / length) ** 2


def halves(table):
    table = np.asarray(table, np.float32)
    high = table.astype(BF16)
    low = (table - high.astype(np.float32)).astype(BF16)
    return np.stack([high, low])


def make_tables():
    side = cas(SIDE)
    spread = np.zeros((LANES, 512))
    for k in range(4):
        spread[96 * k : 96 * k + 96, 128 * k : 128 * k + 96] = side
    order = np.array([4 * h + k for k in range(4) for h in range(ROWS)])
    down = side[:, order]
    square = sine_square(SIDE)
    plane = np.zeros((NX, 9, 128), np.float32)
    lane = np.arange(128)
    for owner in range(NX):
        for i in range(9):
            tile = 9 * (owner // 16) + i
            row = (tile // 3) * 8 + (owner // 2) % 8
            part = tile % 3
            column = np.where(lane < 96, lane, 32 * part + lane - 96)
            plane[owner, i] = square[row] + square[column]
    along = np.broadcast_to(sine_square(NX)[:, None], (NX, 128)).astype(np.float32)
    return (
        halves(spread),
        halves(spread.T),
        halves(down),
        halves(down.T),
        halves(cas(NX)),
        plane,
        np.ascontiguousarray(along),
    )


def split(x):
    high = x.astype(BF16)
    return high, (x - high.astype(F32)).astype(BF16)


def dot(a, b):
    return jnp.dot(a, b, preferred_element_type=F32)


def data_times(x, table):
    high, low = split(x)
    return dot(high, table[0]) + (dot(low, table[0]) + dot(high, table[1]))


def times_data(table, x):
    high, low = split(x)
    return dot(table[0], high) + (dot(table[0], low) + dot(table[1], high))


def projected(get):
    im0, im1, im2 = get(1, 0, 0), get(1, 1, 1), get(1, 2, 2)
    third = (im0 + im1 + im2) * (1.0 / 3.0)
    out = [im0 - third, im1 - third]
    for i, j in ((0, 1), (0, 2), (1, 2)):
        out.append(0.5 * (get(0, i, j) - get(0, j, i)))
        out.append(0.5 * (get(1, i, j) + get(1, j, i)))
    return out


def cayley(a):
    h0, h1, q01, p01, q02, p02, q12, p12 = a
    h2 = -(h0 + h1)
    s01 = p01 * p01 + q01 * q01
    s02 = p02 * p02 + q02 * q02
    s12 = p12 * p12 + q12 * q12
    t0, t1, t2 = h0 * h0, h1 * h1, h2 * h2
    plus = 1.0 + (0.5 * (t0 + t1 + t2) + (s01 + s02 + s12))
    mr = p01 * p12 - q01 * q12
    mi = -(p01 * q12 + q01 * p12)
    nr = p02 * p12 + q02 * q12
    ni = p02 * q12 - q02 * p12
    kr = p01 * p02 + q01 * q02
    ki = q01 * p02 - p01 * q02
    delta = h0 * h1 * h2 + 2.0 * (mr * p02 - mi * q02) - (h0 * s12 + h1 * s02 + h2 * s01)
    scale = 2.0 / (plus * plus + delta * delta)
    u = plus * scale
    v = -delta * scale
    real = [[None] * 3 for _ in range(3)]
    imag = [[None] * 3 for _ in range(3)]
    for i, (h, b) in enumerate(
        (
            (h0, plus - (t0 + s01 + s02)),
            (h1, plus - (t1 + s01 + s12)),
            (h2, plus - (t2 + s02 + s12)),
        )
    ):
        real[i][i] = u * b - v * h - 1.0
        imag[i][i] = u * h + v * b
    for i, j, p, q, br, bi in (
        (0, 1, p01, q01, h2 * p01 - nr, -h2 * q01 - ni),
        (0, 2, p02, q02, h1 * p02 - mr, -h1 * q02 - mi),
        (1, 2, p12, q12, h0 * p12 - kr, -h0 * q12 - ki),
    ):
        ur, ui = br + q, bi + p
        lr, li = br - q, p - bi
        real[i][j] = u * ur - v * ui
        imag[i][j] = u * ui + v * ur
        real[j][i] = u * lr - v * li
        imag[j][i] = u * li + v * lr
    return [real[i][j] for i in range(3) for j in range(3)] + [imag[i][j] for i in range(3) for j in range(3)]


def product(a, b):
    real, imag = [], []
    for i in range(3):
        for j in range(3):
            r = m = None
            for k in range(3):
                ar, ai = a[3 * i + k], a[9 + 3 * i + k]
                br, bi = b[3 * k + j], b[9 + 3 * k + j]
                x, y = ar * br - ai * bi, ar * bi + ai * br
                r, m = (x, y) if r is None else (r + x, m + y)
            real.append(r)
            imag.append(m)
    return real + imag


def product_dagger(a, b):
    real, imag = [], []
    for i in range(3):
        for j in range(3):
            r = m = None
            for k in range(3):
                ar, ai = a[3 * i + k], a[9 + 3 * i + k]
                br, bi = b[3 * j + k], b[9 + 3 * j + k]
                x, y = ar * br + ai * bi, ai * br - ar * bi
                r, m = (x, y) if r is None else (r + x, m + y)
            real.append(r)
            imag.append(m)
    return real + imag


def forward_modes(fields, spread, down, tiles_ref, q):
    part = data_times(fields, spread)
    stacked = jnp.concatenate(
        [
            jnp.concatenate([part[24 * f : 24 * f + 24, 128 * k : 128 * k + 128] for f in range(4)], axis=1)
            for k in range(4)
        ],
        axis=0,
    )
    modes = times_data(down, stacked)
    lane = lax.broadcasted_iota(jnp.int32, (SIDE, 128), 1)
    last = modes[:, 384:]
    for j in range(3):
        tile = jnp.where(lane < 96, modes[:, 128 * j : 128 * j + 128], pltpu.roll(last, 96 - 32 * j, 1))
        for b in range(12):
            tiles_ref[36 * q + 3 * b + j] = tile[8 * b : 8 * b + 8]


def inverse_fields(tiles_ref, spread_t, down_t, halves):
    lane = lax.broadcasted_iota(jnp.int32, (SIDE, 128), 1)
    blocks = []
    for q in halves:
        tiles = [
            jnp.concatenate([tiles_ref[36 * q + 3 * b + j] for b in range(12)], axis=0) for j in range(3)
        ]
        rolled = [pltpu.roll(tiles[j], 32 * j + 32, 1) for j in range(3)]
        last = jnp.where(lane < 32, rolled[0], jnp.where(lane < 64, rolled[1], rolled[2]))
        blocks += tiles + [last]
    stacked = times_data(down_t, jnp.concatenate(blocks, axis=1))
    part = jnp.concatenate(
        [
            jnp.concatenate([stacked[24 * k : 24 * k + 24, 128 * f : 128 * f + 128] for k in range(4)], axis=1)
            for f in range(4 * len(halves))
        ],
        axis=0,
    )
    return data_times(part, spread_t)


def row_turned(x, shift):
    count = x.shape[0] // ROWS
    return pltpu.roll(x.reshape(count, ROWS, x.shape[1]), shift, 1).reshape(x.shape)


def lane_of(x):
    return lax.broadcasted_iota(jnp.int32, x.shape, 1)


def from_y_before(x):
    turned = pltpu.roll(x, 96, 1)
    return jnp.where(lane_of(x) < 96, row_turned(turned, 1), turned)


def from_z_before(x):
    return jnp.where(lane_of(x) % 96 == 0, pltpu.roll(x, LANES - 95, 1), pltpu.roll(x, 1, 1))


def from_y_after(x):
    turned = pltpu.roll(x, LANES - 96, 1)
    return jnp.where(lane_of(x) >= 288, row_turned(turned, ROWS - 1), turned)


def from_z_after(x):
    return jnp.where(lane_of(x) % 96 == 95, pltpu.roll(x, 95, 1), pltpu.roll(x, LANES - 1, 1))


def chips():
    def hops(step):
        return min(step[0], 4 - step[0]) + min(step[1], 8 - step[1])

    steps = [(dx, dy) for dx in range(4) for dy in range(8) if dx or dy]
    return sorted(steps, key=lambda step: (-hops(step), step[1], step[0]))


def kernel(
    u_hbm, spread_hbm, spread_t_hbm, down_hbm, down_t_hbm, along_hbm, plane_hbm, square_hbm,
    out, drift_ref,
    u, spread, spread_t, down, down_t, along, plane, square_x,
    own, prev, rest, snd, rcv, sol, back, ahead, part, parts,
    g, gy, gz, gx, act,
    local_sem, edge_send, edge_recv, onward_send, onward_recv, far_send, far_recv, relay,
):
    me = lax.axis_index("gx")
    x, y, c = me // 16, (me // 2) % 8, me % 2
    after, before = (me + 1) % NX, (me + NX - 1) % NX

    def device(dx, dy, core):
        return ((x + dx) % 4) * 16 + ((y + dy) % 8) * 2 + core

    barrier = pltpu.get_barrier_semaphore()

    def signal(sem, peer):
        pl.semaphore_signal(sem, inc=1, device_id={"gx": peer}, device_id_type=MESH)

    edge_left = jnp.logical_and(y == 0, c == 0)
    edge_right = jnp.logical_and(y == 7, c == 1)
    signal(barrier, device(0, 0, 1 - c))
    for core in range(2):
        for dx, dy in ((0, 1), (0, 7), (1, 0), (3, 0)):
            signal(barrier, device(dx, dy, core))

    @pl.when(edge_left)
    def _():
        signal(barrier, before)

    @pl.when(edge_right)
    def _():
        signal(barrier, after)

    loads = [
        pltpu.make_async_copy(u_hbm.at[pl.ds(18 * d, 18)], u.at[pl.ds(18 * d, 18)], local_sem.at[d])
        for d in range(3)
    ]
    for i, (source, target) in enumerate(
        (
            (spread_hbm, spread), (down_hbm, down), (plane_hbm.at[me], plane), (square_hbm, square_x),
            (along_hbm, along), (down_t_hbm, down_t), (spread_t_hbm, spread_t),
        )
    ):
        loads.append(pltpu.make_async_copy(source, target, local_sem.at[3 + i]))
    for load in loads:
        load.start()

    def project(d, into):
        for j in range(3):
            fields = projected(
                lambda p, a, b: u[18 * d + 9 * p + 3 * a + b, pl.ds(j, ROWS, stride=3), :]
            )
            for f in range(8):
                into[pl.ds(ROWS * f, ROWS), pl.ds(128 * j, 128)] = fields[f]

    loads[0].wait()
    project(0, own)

    pl.semaphore_wait(barrier, 9 + jnp.where(jnp.logical_or(edge_left, edge_right), 1, 0))
    edges = [
        pltpu.make_async_remote_copy(
            src_ref=own.at[pl.ds(96 * q, 96)], dst_ref=prev.at[pl.ds(96 * q, 96)],
            send_sem=edge_send.at[q], recv_sem=edge_recv.at[q],
            device_id={"gx": after}, device_id_type=MESH,
        )
        for q in range(2)
    ]
    for edge in edges:
        edge.start()
    for dx in (1, 3):
        signal(relay.at[0], device(dx, 0, c))

    loads[1].wait()
    project(1, act)
    pl.semaphore_wait(relay.at[0], 2)
    for dy in (1, 7):
        signal(relay.at[1], device(0, dy, c))
    middle = act[...]
    rest[...] = from_y_before(middle) - middle - own[...]
    loads[2].wait()
    project(2, act)
    pl.semaphore_wait(relay.at[1], 2)
    for dx in (0, 1, 3):
        for dy in (2, 6):
            signal(relay.at[2], device(dx, dy, c))
    middle = act[...]
    rest[...] += from_z_before(middle) - middle
    for load in loads[3:]:
        load.wait()

    factor = PEAK_SQUARE * STEP_SIZE * 0.5 / (NX * CELLS)
    filters = []
    for i in range(9):
        square = square_x[...] + plane[pl.ds(i, 1), :]
        positive = square > 0.0
        filters.append(jnp.where(positive, factor / jnp.where(positive, square, 1.0), 0.0))
    filters = jnp.concatenate(filters, axis=1)

    def place(core, chip):
        return pl.ds(36 * core + 9 * (chip // 8), 9), chip % 8

    def there(peer, core):
        return pltpu.make_async_remote_copy(
            src_ref=snd.at[place(core, peer // 2)], dst_ref=rcv.at[:, me],
            send_sem=far_send.at[0], recv_sem=far_recv.at[0],
            device_id={"gx": peer}, device_id_type=MESH,
        )

    partial = None
    for q in range(2):
        edges[q].wait_recv()
        rows = pl.ds(96 * q, 96)
        fields = rest[rows, :] + prev[rows, :]
        tail = fields[48:] if q == 0 else fields
        total = 2.0 * jnp.sum(tail * tail, axis=0, keepdims=True)
        if q == 0:
            f0, f1 = fields[:24], fields[24:48]
            both = f0 + f1
            total += jnp.sum(f0 * f0 + f1 * f1 + both * both, axis=0, keepdims=True)
        partial = total if partial is None else partial + total
        forward_modes(fields, spread, down, snd, q)
        if q == 0:
            pl.semaphore_wait(relay.at[2], 6)
        for dx, dy in chips():
            there(device(dx, dy, q), q).start()

        @pl.when(c != q)
        def _():
            there(device(0, 0, q), q).start()

        @pl.when(c == q)
        def _():
            pltpu.make_async_copy(snd.at[place(q, me // 2)], rcv.at[:, me], far_recv.at[0]).start()

    partial = partial[:, :128] + partial[:, 128:256] + partial[:, 256:]
    part[...] = jnp.broadcast_to(partial, (8, 128))

    def share(k, carry):
        pltpu.make_async_remote_copy(
            src_ref=part.at[0], dst_ref=parts.at[me], send_sem=far_send.at[2], recv_sem=far_recv.at[2],
            device_id={"gx": (me + k) % NX}, device_id_type=MESH,
        ).start()
        return carry

    lax.fori_loop(1, NX, share, 0)
    pltpu.make_async_copy(part.at[0], parts.at[me], far_recv.at[2]).start()

    def arrived(ref, sem):
        pltpu.make_async_copy(ref, ref, sem).wait()

    arrived(rcv, far_recv.at[0])
    waves = times_data(along, jnp.concatenate([rcv[i] for i in range(9)], axis=1))
    waves = times_data(along, waves * filters)
    for i in range(9):
        sol[i] = waves[:, 128 * i : 128 * i + 128]

    tiles, line = place(c, me // 2)
    for dx, dy in chips() + [(0, 0)]:
        for core in range(2):
            peer = device(dx, dy, core if dx or dy else 1 - c)
            if not (dx or dy) and core:
                continue
            pltpu.make_async_remote_copy(
                src_ref=sol.at[:, peer], dst_ref=back.at[tiles, line],
                send_sem=far_send.at[1], recv_sem=far_recv.at[1],
                device_id={"gx": peer}, device_id_type=MESH,
            ).start()
    pltpu.make_async_copy(sol.at[:, me], back.at[tiles, line], far_recv.at[1]).start()

    arrived(parts, far_recv.at[2])
    drift_ref[0] = jnp.sum(parts[...]) * (1.0 / (9.0 * NX * CELLS))
    arrived(rcv.at[:, pl.ds(0, NX - 1)], far_send.at[0])
    arrived(parts.at[pl.ds(0, NX - 1)], far_send.at[2])
    for edge in edges:
        edge.wait_send()

    arrived(back, far_recv.at[1])
    onward = [
        pltpu.make_async_remote_copy(
            src_ref=back.at[pl.ds(36 * q, 36)], dst_ref=ahead.at[pl.ds(36 * q, 36)],
            send_sem=onward_send.at[q], recv_sem=onward_recv.at[q],
            device_id={"gx": before}, device_id_type=MESH,
        )
        for q in range(2)
    ]
    for half in onward:
        half.start()

    def chunks(action):
        def body(k, carry):
            i, t = k // 3, k % 3
            r, j = pl.multiple_of(8 * i, 8), pl.multiple_of(128 * t, 128)
            action(
                lambda ref, count: [ref[pl.ds(ROWS * e + r, 8), pl.ds(j, 128)] for e in range(count)],
                lambda ref, e: (ROWS * e + r, j),
                pl.ds(24 * i + t, 8, stride=3),
            )
            return carry

        lax.fori_loop(0, 9, body, 0)

    def rotate(into):
        def action(read, at, sites):
            entries = cayley(read(act, 8))
            for e in range(18):
                r, j = at(into, e)
                into[pl.ds(r, 8), pl.ds(j, 128)] = entries[e]

        chunks(action)

    act[...] = inverse_fields(back, spread_t, down_t, (0, 1))
    rotate(g)
    whole = g[...]
    gy[...] = from_y_after(whole)
    gz[...] = from_z_after(whole)

    def update(read, at, sites):
        left = read(g, 18)
        for d, aheads in ((1, gy), (2, gz)):
            links = [u[18 * d + e, sites, :] for e in range(18)]
            new = product_dagger(product(left, links), read(aheads, 18))
            for e in range(18):
                out[18 * d + e, sites, :] = new[e]
        new = product(left, [u[e, sites, :] for e in range(18)])
        for e in range(18):
            r, j = at(gx, e)
            gx[pl.ds(r, 8), pl.ds(j, 128)] = new[e]

    chunks(update)

    for q in range(2):
        onward[q].wait_recv()
        act[pl.ds(96 * q, 96), :] = inverse_fields(ahead, spread_t, down_t, (q,))

    def finish(read, at, sites):
        new = product_dagger(read(gx, 18), cayley(read(act, 8)))
        for e in range(18):
            out[e, sites, :] = new[e]

    chunks(finish)
    arrived(rcv.at[:, pl.ds(0, NX - 1)], far_send.at[1])
    for half in onward:
        half.wait_send()


def local(gauge_links):
    tables = [jnp.asarray(t) for t in make_tables()]
    hbm = pl.BlockSpec(memory_space=pltpu.HBM)
    dma = pltpu.SemaphoreType.DMA
    fields = pltpu.VMEM((8 * ROWS, LANES), F32)
    matrix = pltpu.VMEM((18 * ROWS, LANES), F32)
    tiles = pltpu.VMEM((72, 8, 128), F32)
    waves = pltpu.VMEM((9, NX, 128), F32)
    links, drift = pl.pallas_call(
        kernel,
        out_shape=(
            pltpu.VMEM((54, 72, 128), F32),
            jax.ShapeDtypeStruct((1,), F32),
        ),
        in_specs=[hbm] * 8,
        out_specs=(pl.BlockSpec(memory_space=pltpu.VMEM), pl.BlockSpec(memory_space=pltpu.SMEM)),
        scratch_shapes=[
            pltpu.VMEM((54, 72, 128), F32),
            pltpu.VMEM((2, LANES, 512), BF16),
            pltpu.VMEM((2, 512, LANES), BF16),
            pltpu.VMEM((2, SIDE, SIDE), BF16),
            pltpu.VMEM((2, SIDE, SIDE), BF16),
            pltpu.VMEM((2, NX, NX), BF16),
            pltpu.VMEM((9, 128), F32),
            pltpu.VMEM((NX, 128), F32),
            fields, fields, fields,
            tiles, waves, waves, tiles, tiles,
            pltpu.VMEM((8, 128), F32),
            pltpu.VMEM((NX, 128), F32),
            matrix, matrix, matrix, matrix,
            fields,
            dma((10,)), dma((2,)), dma((2,)), dma((2,)), dma((2,)), dma((3,)), dma((3,)),
            pltpu.SemaphoreType.REGULAR((3,)),
        ],
        compiler_params=pltpu.CompilerParams(
            collective_id=0, has_side_effects=True, vmem_limit_bytes=24 << 20
        ),
    )(*[pltpu.with_memory_space_constraint(t, pltpu.HBM) for t in (gauge_links.reshape(54, 72, 128), *tables)])
    return links.reshape(gauge_links.shape), drift


def solution(mesh):
    split_x = ("ta", "gx")
    return jax.shard_map(
        local,
        mesh=mesh,
        in_specs=(P(None, None, None, None, split_x, None),),
        out_specs=(P(None, None, None, None, split_x, None), P("ta")),
        check_vma=False,
    )
```

```python
import math

import jax
import jax.numpy as jnp
import numpy as np
from jax import lax
from jax.experimental import pallas as pl
from jax.experimental.pallas import tpu as pltpu
from jax.sharding import PartitionSpec as P

SIDE = 96
NX = 64
CELLS = SIDE * SIDE
ROWS, LANES = 24, 384
STEP_SIZE = 0.08
PEAK_SQUARE = 12.0
MESH = pl.DeviceIdType.MESH
F32 = jnp.float32
BF16 = jnp.bfloat16


def cas(length):
    index = np.arange(length)
    angle = 2.0 * np.pi * ((index[:, None] * index[None, :]) % length) / length
    return np.cos(angle) + np.sin(angle)


def sine_square(length):
    return 4.0 * np.sin(np.pi * np.arange(length) / length) ** 2


def halves(table):
    table = np.asarray(table, np.float32)
    high = table.astype(BF16)
    low = (table - high.astype(np.float32)).astype(BF16)
    return np.stack([high, low])


def make_tables():
    side = cas(SIDE)
    spread = np.zeros((LANES, 512))
    for k in range(4):
        spread[96 * k : 96 * k + 96, 128 * k : 128 * k + 96] = side
    order = np.array([4 * h + k for k in range(4) for h in range(ROWS)])
    down = side[:, order]
    square = sine_square(SIDE)
    plane = np.zeros((NX, 9, 128), np.float32)
    lane = np.arange(128)
    for owner in range(NX):
        for i in range(9):
            tile = 9 * (owner // 16) + i
            row = (tile // 3) * 8 + (owner // 2) % 8
            part = tile % 3
            column = np.where(lane < 96, lane, 32 * part + lane - 96)
            plane[owner, i] = square[row] + square[column]
    along = np.broadcast_to(sine_square(NX)[:, None], (NX, 128)).astype(np.float32)
    return (
        halves(spread),
        halves(spread.T),
        halves(down).reshape(2 * SIDE, SIDE),
        halves(down.T).reshape(2 * SIDE, SIDE),
        halves(cas(NX)).reshape(2 * NX, NX),
        plane,
        np.ascontiguousarray(along),
    )


def split(x):
    high = x.astype(BF16)
    return high, (x - high.astype(F32)).astype(BF16)


def dot(a, b):
    return jnp.dot(a, b, preferred_element_type=F32)


def data_times(x, table):
    high, low = split(x)
    rows = x.shape[0]
    both = dot(jnp.concatenate([high, low], axis=0), table[0])
    return both[:rows] + (both[rows:] + dot(high, table[1]))


def times_data(table, x):
    high, low = split(x)
    rows = table.shape[0] // 2
    both = dot(table[...], high)
    return both[:rows] + (both[rows:] + dot(table[:rows], low))


def projected(get):
    im0, im1, im2 = get(1, 0, 0), get(1, 1, 1), get(1, 2, 2)
    third = (im0 + im1 + im2) * (1.0 / 3.0)
    out = [im0 - third, im1 - third]
    for i, j in ((0, 1), (0, 2), (1, 2)):
        out.append(0.5 * (get(0, i, j) - get(0, j, i)))
        out.append(0.5 * (get(1, i, j) + get(1, j, i)))
    return out


def cayley(a):
    h0, h1, q01, p01, q02, p02, q12, p12 = a
    h2 = -(h0 + h1)
    s01 = p01 * p01 + q01 * q01
    s02 = p02 * p02 + q02 * q02
    s12 = p12 * p12 + q12 * q12
    t0, t1, t2 = h0 * h0, h1 * h1, h2 * h2
    plus = 1.0 + (0.5 * (t0 + t1 + t2) + (s01 + s02 + s12))
    mr = p01 * p12 - q01 * q12
    mi = -(p01 * q12 + q01 * p12)
    nr = p02 * p12 + q02 * q12
    ni = p02 * q12 - q02 * p12
    kr = p01 * p02 + q01 * q02
    ki = q01 * p02 - p01 * q02
    delta = h0 * h1 * h2 + 2.0 * (mr * p02 - mi * q02) - (h0 * s12 + h1 * s02 + h2 * s01)
    scale = 2.0 / (plus * plus + delta * delta)
    u = plus * scale
    v = -delta * scale
    real = [[None] * 3 for _ in range(3)]
    imag = [[None] * 3 for _ in range(3)]
    for i, (h, b) in enumerate(
        (
            (h0, plus - (t0 + s01 + s02)),
            (h1, plus - (t1 + s01 + s12)),
            (h2, plus - (t2 + s02 + s12)),
        )
    ):
        real[i][i] = u * b - v * h - 1.0
        imag[i][i] = u * h + v * b
    for i, j, p, q, br, bi in (
        (0, 1, p01, q01, h2 * p01 - nr, -h2 * q01 - ni),
        (0, 2, p02, q02, h1 * p02 - mr, -h1 * q02 - mi),
        (1, 2, p12, q12, h0 * p12 - kr, -h0 * q12 - ki),
    ):
        ur, ui = br + q, bi + p
        lr, li = br - q, p - bi
        real[i][j] = u * ur - v * ui
        imag[i][j] = u * ui + v * ur
        real[j][i] = u * lr - v * li
        imag[j][i] = u * li + v * lr
    return [real[i][j] for i in range(3) for j in range(3)] + [imag[i][j] for i in range(3) for j in range(3)]


def product(a, b):
    real, imag = [], []
    for i in range(3):
        for j in range(3):
            r = m = None
            for k in range(3):
                ar, ai = a[3 * i + k], a[9 + 3 * i + k]
                br, bi = b[3 * k + j], b[9 + 3 * k + j]
                x, y = ar * br - ai * bi, ar * bi + ai * br
                r, m = (x, y) if r is None else (r + x, m + y)
            real.append(r)
            imag.append(m)
    return real + imag


def product_dagger(a, b):
    real, imag = [], []
    for i in range(3):
        for j in range(3):
            r = m = None
            for k in range(3):
                ar, ai = a[3 * i + k], a[9 + 3 * i + k]
                br, bi = b[3 * j + k], b[9 + 3 * j + k]
                x, y = ar * br + ai * bi, ai * br - ar * bi
                r, m = (x, y) if r is None else (r + x, m + y)
            real.append(r)
            imag.append(m)
    return real + imag


def forward_modes(fields, spread, down, tiles_ref, q):
    part = data_times(fields, spread)
    stacked = jnp.concatenate(
        [
            jnp.concatenate([part[24 * f : 24 * f + 24, 128 * k : 128 * k + 128] for f in range(4)], axis=1)
            for k in range(4)
        ],
        axis=0,
    )
    modes = times_data(down, stacked)
    lane = lax.broadcasted_iota(jnp.int32, (SIDE, 128), 1)
    last = modes[:, 384:]
    for j in range(3):
        tile = jnp.where(lane < 96, modes[:, 128 * j : 128 * j + 128], pltpu.roll(last, 96 - 32 * j, 1))
        for b in range(12):
            tiles_ref[36 * q + 3 * b + j] = tile[8 * b : 8 * b + 8]


def inverse_fields(tiles_ref, spread_t, down_t, halves):
    lane = lax.broadcasted_iota(jnp.int32, (SIDE, 128), 1)
    blocks = []
    for q in halves:
        tiles = [
            jnp.concatenate([tiles_ref[36 * q + 3 * b + j] for b in range(12)], axis=0) for j in range(3)
        ]
        rolled = [pltpu.roll(tiles[j], 32 * j + 32, 1) for j in range(3)]
        last = jnp.where(lane < 32, rolled[0], jnp.where(lane < 64, rolled[1], rolled[2]))
        blocks += tiles + [last]
    stacked = times_data(down_t, jnp.concatenate(blocks, axis=1))
    part = jnp.concatenate(
        [
            jnp.concatenate([stacked[24 * k : 24 * k + 24, 128 * f : 128 * f + 128] for k in range(4)], axis=1)
            for f in range(4 * len(halves))
        ],
        axis=0,
    )
    return data_times(part, spread_t)


def row_turned(x, shift):
    count = x.shape[0] // ROWS
    return pltpu.roll(x.reshape(count, ROWS, x.shape[1]), shift, 1).reshape(x.shape)


def lane_of(x):
    return lax.broadcasted_iota(jnp.int32, x.shape, 1)


def from_y_before(x):
    turned = pltpu.roll(x, 96, 1)
    first = turned[:, :128]
    first = jnp.where(lane_of(first) < 96, row_turned(first, 1), first)
    return jnp.concatenate([first, turned[:, 128:]], axis=1)


def from_z_before(x):
    return jnp.where(lane_of(x) % 96 == 0, pltpu.roll(x, LANES - 95, 1), pltpu.roll(x, 1, 1))


def from_y_after(x):
    turned = pltpu.roll(x, LANES - 96, 1)
    last = turned[:, 256:]
    last = jnp.where(lane_of(last) >= 32, row_turned(last, ROWS - 1), last)
    return jnp.concatenate([turned[:, :256], last], axis=1)


def from_z_after(x):
    return jnp.where(lane_of(x) % 96 == 95, pltpu.roll(x, 95, 1), pltpu.roll(x, LANES - 1, 1))


def chips():
    def hops(step):
        return min(step[0], 4 - step[0]) + min(step[1], 8 - step[1])

    steps = [(dx, dy) for dx in range(4) for dy in range(8) if dx or dy]
    return sorted(steps, key=lambda step: (-hops(step), step[1], step[0]))


EARLY = ((4,), (3, 5), (2, 6))
LATE = (0, 1, 7)


def kernel(
    u_hbm, spread_hbm, spread_t_hbm, down_hbm, down_t_hbm, along_hbm, plane_hbm, square_hbm,
    out, drift_ref,
    u, spread, spread_t, down, down_t, along, plane, square_x,
    own, prev, rest, snd, rcv, sol, back, ahead, part, parts, total_ref,
    g, gy, gz, gx, act,
    local_sem, edge_send, edge_recv, onward_send, onward_recv, far_send, far_recv, relay,
):
    me = lax.axis_index("gx")
    x, y, c = me // 16, (me // 2) % 8, me % 2
    after, before = (me + 1) % NX, (me + NX - 1) % NX

    def device(dx, dy, core):
        return ((x + dx) % 4) * 16 + ((y + dy) % 8) * 2 + core

    barrier = pltpu.get_barrier_semaphore()

    def signal(sem, peer):
        pl.semaphore_signal(sem, inc=1, device_id={"gx": peer}, device_id_type=MESH)

    loads = [
        pltpu.make_async_copy(u_hbm.at[pl.ds(18 * d, 18)], u.at[pl.ds(18 * d, 18)], local_sem.at[d])
        for d in range(3)
    ]
    for i, (source, target) in enumerate(
        (
            (spread_hbm, spread), (down_hbm, down), (plane_hbm.at[me], plane), (square_hbm, square_x),
            (along_hbm, along), (down_t_hbm, down_t), (spread_t_hbm, spread_t),
        )
    ):
        loads.append(pltpu.make_async_copy(source, target, local_sem.at[3 + i]))
    loads[0].start()

    edge_left = jnp.logical_and(y == 0, c == 0)
    edge_right = jnp.logical_and(y == 7, c == 1)
    signal(barrier, device(0, 0, 1 - c))
    for core in range(2):
        for dx, dy in ((0, 1), (0, 7), (1, 0), (3, 0)):
            signal(barrier, device(dx, dy, core))

    @pl.when(edge_left)
    def _():
        signal(barrier, before)

    @pl.when(edge_right)
    def _():
        signal(barrier, after)

    for load in loads[1:]:
        load.start()

    def project(d, into):
        for j in range(3):
            fields = projected(
                lambda p, a, b: u[18 * d + 9 * p + 3 * a + b, pl.ds(j, ROWS, stride=3), :]
            )
            for f in range(8):
                into[pl.ds(ROWS * f, ROWS), pl.ds(128 * j, 128)] = fields[f]

    def entered():
        pl.semaphore_wait(barrier, 9 + jnp.where(jnp.logical_or(edge_left, edge_right), 1, 0))

    loads[0].wait()
    project(0, own)
    entered()
    edges = [
        pltpu.make_async_remote_copy(
            src_ref=own.at[pl.ds(96 * q, 96)], dst_ref=prev.at[pl.ds(96 * q, 96)],
            send_sem=edge_send.at[q], recv_sem=edge_recv.at[q],
            device_id={"gx": after}, device_id_type=MESH,
        )
        for q in range(2)
    ]
    for edge in edges:
        edge.start()
    for dx in (1, 3):
        signal(relay.at[0], device(dx, 0, c))
    pl.semaphore_wait(relay.at[0], 2)
    for dy in (1, 7):
        signal(relay.at[1], device(0, dy, c))
    pl.semaphore_wait(relay.at[1], 2)
    for dx in (0, 1, 3):
        for dy in (2, 6):
            signal(relay.at[2], device(dx, dy, c))

    loads[1].wait()
    project(1, act)
    middle = act[...]
    rest[...] = from_y_before(middle) - middle - own[...]
    loads[2].wait()
    project(2, act)
    middle = act[...]
    rest[...] += from_z_before(middle) - middle
    for load in loads[3:]:
        load.wait()

    factor = PEAK_SQUARE * STEP_SIZE * 0.5 / (NX * CELLS)
    filters = []
    for i in range(9):
        square = square_x[...] + plane[pl.ds(i, 1), :]
        positive = square > 0.0
        filters.append(jnp.where(positive, factor / jnp.where(positive, square, 1.0), 0.0))
    filters = jnp.concatenate(filters, axis=1)

    def place(core, chip):
        return pl.ds(36 * core + 9 * (chip // 8), 9), chip % 8

    def there(peer, core):
        return pltpu.make_async_remote_copy(
            src_ref=snd.at[place(core, peer // 2)], dst_ref=rcv.at[:, me],
            send_sem=far_send.at[0], recv_sem=far_recv.at[0],
            device_id={"gx": peer}, device_id_type=MESH,
        )

    def arrived(ref, sem):
        pltpu.make_async_copy(ref, ref, sem).wait()

    partial = None
    for q in range(2):
        edges[q].wait_recv()
        rows = pl.ds(96 * q, 96)
        fields = rest[rows, :] + prev[rows, :]
        tail = fields[48:] if q == 0 else fields
        total = 2.0 * jnp.sum(tail * tail, axis=0, keepdims=True)
        if q == 0:
            f0, f1 = fields[:24], fields[24:48]
            both = f0 + f1
            total += jnp.sum(f0 * f0 + f1 * f1 + both * both, axis=0, keepdims=True)
        partial = total if partial is None else partial + total
        forward_modes(fields, spread, down, snd, q)
        if q == 0:
            pl.semaphore_wait(relay.at[2], 6)
        for dx, dy in chips():
            there(device(dx, dy, q), q).start()

        @pl.when(c != q)
        def _():
            there(device(0, 0, q), q).start()

        @pl.when(c == q)
        def _():
            pltpu.make_async_copy(snd.at[place(q, me // 2)], rcv.at[:, me], far_recv.at[0]).start()

    partial = partial[:, :128] + partial[:, 128:256] + partial[:, 256:]
    part[0] = jnp.broadcast_to(partial, (8, 128))

    def share(stage, row, peers):
        for peer in peers:
            pltpu.make_async_remote_copy(
                src_ref=part.at[stage], dst_ref=parts.at[stage, row],
                send_sem=far_send.at[2 + stage], recv_sem=far_recv.at[2 if stage == 0 else 6],
                device_id={"gx": peer}, device_id_type=MESH,
            ).start()
        pltpu.make_async_copy(
            part.at[stage], parts.at[stage, row], far_recv.at[2 if stage == 0 else 6]
        ).start()

    share(0, y, [device(0, dy, c) for dy in range(1, 8)])


    arrived(rcv, far_recv.at[0])
    waves = times_data(along, jnp.concatenate([rcv[i] for i in range(9)], axis=1))
    waves = times_data(along, waves * filters)
    for i in range(9):
        sol[i] = waves[:, 128 * i : 128 * i + 128]

    tiles, line = place(c, me // 2)
    came = {dy: 3 + i for i, group in enumerate(EARLY) for dy in group}
    for dx, dy in chips() + [(0, 0)]:
        for core in range(2):
            peer = device(dx, dy, core if dx or dy else 1 - c)
            if not (dx or dy) and core:
                continue
            pltpu.make_async_remote_copy(
                src_ref=sol.at[:, peer], dst_ref=back.at[tiles, line],
                send_sem=far_send.at[1], recv_sem=far_recv.at[1 if dy in LATE else came[dy]],
                device_id={"gx": peer}, device_id_type=MESH,
            ).start()
    pltpu.make_async_copy(sol.at[:, me], back.at[tiles, line], far_recv.at[1]).start()

    arrived(parts.at[0], far_recv.at[2])
    part[1] = jnp.broadcast_to(jnp.sum(parts[0, :, 0, :], axis=0, keepdims=True), (8, 128))
    share(1, 2 * x + c, [device(dx, 0, core) for dx in range(1, 4) for core in range(2)] + [device(0, 0, 1 - c)])
    arrived(rcv.at[:, pl.ds(0, NX - 1)], far_send.at[0])
    arrived(parts.at[0, pl.ds(0, 7)], far_send.at[2])
    for edge in edges:
        edge.wait_send()

    def onward(part, dy, sem):
        rows = (part, (y + dy) % 8)
        pltpu.make_async_remote_copy(
            src_ref=back.at[rows], dst_ref=ahead.at[rows],
            send_sem=onward_send.at[0], recv_sem=onward_recv.at[sem],
            device_id={"gx": before}, device_id_type=MESH,
        ).start()

    for i, group in enumerate(EARLY):
        arrived(back.at[pl.ds(0, 9 * len(group))], far_recv.at[3 + i])
        for dy in group:
            onward(pl.ds(0, 72), dy, 0)
    arrived(back.at[pl.ds(0, 9 * len(LATE))], far_recv.at[1])
    for q in range(2):
        for dy in LATE:
            onward(pl.ds(36 * q, 36), dy, 1 + q)

    def chunks(action):
        def body(k, carry):
            i, t = k // 3, k % 3
            r, j = pl.multiple_of(8 * i, 8), pl.multiple_of(128 * t, 128)
            action(
                lambda ref, count: [ref[pl.ds(ROWS * e + r, 8), pl.ds(j, 128)] for e in range(count)],
                lambda ref, e: (ROWS * e + r, j),
                pl.ds(24 * i + t, 8, stride=3),
            )
            return carry

        lax.fori_loop(0, 9, body, 0)

    def rotate(into):
        def action(read, at, sites):
            entries = cayley(read(act, 8))
            for e in range(18):
                r, j = at(into, e)
                into[pl.ds(r, 8), pl.ds(j, 128)] = entries[e]

        chunks(action)

    act[...] = inverse_fields(back, spread_t, down_t, (0, 1))
    rotate(g)
    whole = g[...]
    gy[...] = from_y_after(whole)
    gz[...] = from_z_after(whole)

    def update(read, at, sites):
        left = read(g, 18)
        for d, aheads in ((1, gy), (2, gz)):
            links = [u[18 * d + e, sites, :] for e in range(18)]
            new = product_dagger(product(left, links), read(aheads, 18))
            for e in range(18):
                out[18 * d + e, sites, :] = new[e]
        new = product(left, [u[e, sites, :] for e in range(18)])
        for e in range(18):
            r, j = at(gx, e)
            gx[pl.ds(r, 8), pl.ds(j, 128)] = new[e]

    chunks(update)

    arrived(ahead.at[pl.ds(0, 72 - 9 * len(LATE))], onward_recv.at[0])
    arrived(parts.at[1], far_recv.at[6])
    total_ref[0] = jnp.sum(parts[1, :, 0, :]) * (1.0 / (9.0 * NX * CELLS))
    drift = pltpu.make_async_copy(total_ref, drift_ref, local_sem.at[0])
    drift.start()

    for q in range(2):
        arrived(snd.at[pl.ds(0, 36), pl.ds(0, len(LATE))], onward_recv.at[1 + q])
        act[pl.ds(96 * q, 96), :] = inverse_fields(ahead, spread_t, down_t, (q,))

    def finish(read, at, sites):
        new = product_dagger(read(gx, 18), cayley(read(act, 8)))
        for e in range(18):
            out[e, sites, :] = new[e]

    chunks(finish)
    arrived(rcv.at[:, pl.ds(0, NX - 1)], far_send.at[1])
    arrived(parts.at[0, pl.ds(0, 7)], far_send.at[3])
    drift.wait()
    arrived(back, onward_send.at[0])


def local(gauge_links):
    tables = [jnp.asarray(t) for t in make_tables()]
    hbm = pl.BlockSpec(memory_space=pltpu.HBM)
    dma = pltpu.SemaphoreType.DMA
    fields = pltpu.VMEM((8 * ROWS, LANES), F32)
    matrix = pltpu.VMEM((18 * ROWS, LANES), F32)
    tiles = pltpu.VMEM((72, 8, 128), F32)
    waves = pltpu.VMEM((9, NX, 128), F32)
    links, drift = pl.pallas_call(
        kernel,
        out_shape=(
            pltpu.VMEM((54, 72, 128), F32),
            jax.ShapeDtypeStruct((1,), F32),
        ),
        in_specs=[hbm] * 8,
        out_specs=(pl.BlockSpec(memory_space=pltpu.VMEM), pl.BlockSpec(memory_space=pl.ANY)),
        scratch_shapes=[
            pltpu.VMEM((54, 72, 128), F32),
            pltpu.VMEM((2, LANES, 512), BF16),
            pltpu.VMEM((2, 512, LANES), BF16),
            pltpu.VMEM((2 * SIDE, SIDE), BF16),
            pltpu.VMEM((2 * SIDE, SIDE), BF16),
            pltpu.VMEM((2 * NX, NX), BF16),
            pltpu.VMEM((9, 128), F32),
            pltpu.VMEM((NX, 128), F32),
            fields, fields, fields,
            tiles, waves, waves, tiles, tiles,
            pltpu.VMEM((2, 8, 128), F32),
            pltpu.VMEM((2, 8, 8, 128), F32),
            pltpu.SMEM((1,), F32),
            matrix, matrix, matrix, matrix,
            fields,
            dma((10,)), dma((2,)), dma((2,)), dma((1,)), dma((3,)), dma((4,)), dma((7,)),
            pltpu.SemaphoreType.REGULAR((3,)),
        ],
        compiler_params=pltpu.CompilerParams(
            collective_id=0, has_side_effects=True, vmem_limit_bytes=24 << 20
        ),
    )(*[pltpu.with_memory_space_constraint(t, pltpu.HBM) for t in (gauge_links.reshape(54, 72, 128), *tables)])
    return links.reshape(gauge_links.shape), drift


def solution(mesh):
    split_x = ("ta", "gx")
    return jax.shard_map(
        local,
        mesh=mesh,
        in_specs=(P(None, None, None, None, split_x, None),),
        out_specs=(P(None, None, None, None, split_x, None), P("ta")),
        check_vma=False,
    )
```

```python
import math

import jax
import jax.numpy as jnp
import numpy as np
from jax import lax
from jax.experimental import pallas as pl
from jax.experimental.pallas import tpu as pltpu
from jax.sharding import PartitionSpec as P

SIDE = 96
NX = 64
CELLS = SIDE * SIDE
ROWS, LANES = 24, 384
STEP_SIZE = 0.08
PEAK_SQUARE = 12.0
MESH = pl.DeviceIdType.MESH
F32 = jnp.float32
BF16 = jnp.bfloat16


def cas(length):
    index = np.arange(length)
    angle = 2.0 * np.pi * ((index[:, None] * index[None, :]) % length) / length
    return np.cos(angle) + np.sin(angle)


def sine_square(length):
    return 4.0 * np.sin(np.pi * np.arange(length) / length) ** 2


def halves(table):
    table = np.asarray(table, np.float32)
    high = table.astype(BF16)
    low = (table - high.astype(np.float32)).astype(BF16)
    return np.stack([high, low])


def make_tables():
    side = cas(SIDE)
    spread = np.zeros((LANES, 512))
    for k in range(4):
        spread[96 * k : 96 * k + 96, 128 * k : 128 * k + 96] = side
    order = np.array([4 * h + k for k in range(4) for h in range(ROWS)])
    down = side[:, order]
    square = sine_square(SIDE)
    plane = np.zeros((NX, 9, 128), np.float32)
    lane = np.arange(128)
    for owner in range(NX):
        for i in range(9):
            tile = 9 * (owner // 16) + i
            row = (tile // 3) * 8 + (owner // 2) % 8
            part = tile % 3
            column = np.where(lane < 96, lane, 32 * part + lane - 96)
            plane[owner, i] = square[row] + square[column]
    along = np.broadcast_to(sine_square(NX)[:, None], (NX, 128)).astype(np.float32)
    return (
        halves(spread),
        halves(spread.T),
        halves(down).reshape(2 * SIDE, SIDE),
        halves(down.T).reshape(2 * SIDE, SIDE),
        halves(cas(NX)).reshape(2 * NX, NX),
        plane,
        np.ascontiguousarray(along),
    )


def split(x):
    high = x.astype(BF16)
    return high, (x - high.astype(F32)).astype(BF16)


def dot(a, b):
    return jnp.dot(a, b, preferred_element_type=F32)


def data_times(x, table):
    high, low = split(x)
    rows = x.shape[0]
    both = dot(jnp.concatenate([high, low], axis=0), table[0])
    return both[:rows] + (both[rows:] + dot(high, table[1]))


def times_data(table, x):
    high, low = split(x)
    rows = table.shape[0] // 2
    both = dot(table[...], high)
    return both[:rows] + (both[rows:] + dot(table[:rows], low))


def projected(get):
    im0, im1, im2 = get(1, 0, 0), get(1, 1, 1), get(1, 2, 2)
    third = (im0 + im1 + im2) * (1.0 / 3.0)
    out = [im0 - third, im1 - third]
    for i, j in ((0, 1), (0, 2), (1, 2)):
        out.append(0.5 * (get(0, i, j) - get(0, j, i)))
        out.append(0.5 * (get(1, i, j) + get(1, j, i)))
    return out


def cayley(a):
    h0, h1, q01, p01, q02, p02, q12, p12 = a
    h2 = -(h0 + h1)
    s01 = p01 * p01 + q01 * q01
    s02 = p02 * p02 + q02 * q02
    s12 = p12 * p12 + q12 * q12
    t0, t1, t2 = h0 * h0, h1 * h1, h2 * h2
    plus = 1.0 + (0.5 * (t0 + t1 + t2) + (s01 + s02 + s12))
    mr = p01 * p12 - q01 * q12
    mi = -(p01 * q12 + q01 * p12)
    nr = p02 * p12 + q02 * q12
    ni = p02 * q12 - q02 * p12
    kr = p01 * p02 + q01 * q02
    ki = q01 * p02 - p01 * q02
    delta = h0 * h1 * h2 + 2.0 * (mr * p02 - mi * q02) - (h0 * s12 + h1 * s02 + h2 * s01)
    scale = 2.0 / (plus * plus + delta * delta)
    u = plus * scale
    v = -delta * scale
    real = [[None] * 3 for _ in range(3)]
    imag = [[None] * 3 for _ in range(3)]
    for i, (h, b) in enumerate(
        (
            (h0, plus - (t0 + s01 + s02)),
            (h1, plus - (t1 + s01 + s12)),
            (h2, plus - (t2 + s02 + s12)),
        )
    ):
        real[i][i] = u * b - v * h - 1.0
        imag[i][i] = u * h + v * b
    for i, j, p, q, br, bi in (
        (0, 1, p01, q01, h2 * p01 - nr, -h2 * q01 - ni),
        (0, 2, p02, q02, h1 * p02 - mr, -h1 * q02 - mi),
        (1, 2, p12, q12, h0 * p12 - kr, -h0 * q12 - ki),
    ):
        ur, ui = br + q, bi + p
        lr, li = br - q, p - bi
        real[i][j] = u * ur - v * ui
        imag[i][j] = u * ui + v * ur
        real[j][i] = u * lr - v * li
        imag[j][i] = u * li + v * lr
    return [real[i][j] for i in range(3) for j in range(3)] + [imag[i][j] for i in range(3) for j in range(3)]


def product(a, b):
    real, imag = [], []
    for i in range(3):
        for j in range(3):
            r = m = None
            for k in range(3):
                ar, ai = a[3 * i + k], a[9 + 3 * i + k]
                br, bi = b[3 * k + j], b[9 + 3 * k + j]
                x, y = ar * br - ai * bi, ar * bi + ai * br
                r, m = (x, y) if r is None else (r + x, m + y)
            real.append(r)
            imag.append(m)
    return real + imag


def product_dagger(a, b):
    real, imag = [], []
    for i in range(3):
        for j in range(3):
            r = m = None
            for k in range(3):
                ar, ai = a[3 * i + k], a[9 + 3 * i + k]
                br, bi = b[3 * j + k], b[9 + 3 * j + k]
                x, y = ar * br + ai * bi, ai * br - ar * bi
                r, m = (x, y) if r is None else (r + x, m + y)
            real.append(r)
            imag.append(m)
    return real + imag


def forward_modes(fields, spread, down, tiles_ref, q):
    part = data_times(fields, spread)
    stacked = jnp.concatenate(
        [
            jnp.concatenate([part[24 * f : 24 * f + 24, 128 * k : 128 * k + 128] for f in range(4)], axis=1)
            for k in range(4)
        ],
        axis=0,
    )
    modes = times_data(down, stacked)
    lane = lax.broadcasted_iota(jnp.int32, (SIDE, 128), 1)
    last = modes[:, 384:]
    for j in range(3):
        tile = jnp.where(lane < 96, modes[:, 128 * j : 128 * j + 128], pltpu.roll(last, 96 - 32 * j, 1))
        for b in range(12):
            tiles_ref[36 * q + 3 * b + j] = tile[8 * b : 8 * b + 8]


def inverse_fields(tiles_ref, spread_t, down_t, halves):
    lane = lax.broadcasted_iota(jnp.int32, (SIDE, 128), 1)
    blocks = []
    for q in halves:
        tiles = [
            jnp.concatenate([tiles_ref[36 * q + 3 * b + j] for b in range(12)], axis=0) for j in range(3)
        ]
        rolled = [pltpu.roll(tiles[j], 32 * j + 32, 1) for j in range(3)]
        last = jnp.where(lane < 32, rolled[0], jnp.where(lane < 64, rolled[1], rolled[2]))
        blocks += tiles + [last]
    stacked = times_data(down_t, jnp.concatenate(blocks, axis=1))
    part = jnp.concatenate(
        [
            jnp.concatenate([stacked[24 * k : 24 * k + 24, 128 * f : 128 * f + 128] for k in range(4)], axis=1)
            for f in range(4 * len(halves))
        ],
        axis=0,
    )
    return data_times(part, spread_t)


def row_turned(x, shift):
    count = x.shape[0] // ROWS
    return pltpu.roll(x.reshape(count, ROWS, x.shape[1]), shift, 1).reshape(x.shape)


def lane_of(x):
    return lax.broadcasted_iota(jnp.int32, x.shape, 1)


def from_y_before(x):
    turned = pltpu.roll(x, 96, 1)
    first = turned[:, :128]
    first = jnp.where(lane_of(first) < 96, row_turned(first, 1), first)
    return jnp.concatenate([first, turned[:, 128:]], axis=1)


def from_z_before(x):
    return jnp.where(lane_of(x) % 96 == 0, pltpu.roll(x, LANES - 95, 1), pltpu.roll(x, 1, 1))


def from_y_after(x):
    turned = pltpu.roll(x, LANES - 96, 1)
    last = turned[:, 256:]
    last = jnp.where(lane_of(last) >= 32, row_turned(last, ROWS - 1), last)
    return jnp.concatenate([turned[:, :256], last], axis=1)


def from_z_after(x):
    return jnp.where(lane_of(x) % 96 == 95, pltpu.roll(x, 95, 1), pltpu.roll(x, LANES - 1, 1))


def chips():
    def hops(step):
        return min(step[0], 4 - step[0]) + min(step[1], 8 - step[1])

    steps = [(dx, dy) for dx in range(4) for dy in range(8) if dx or dy]
    return sorted(steps, key=lambda step: (-hops(step), step[1], step[0]))


EARLY = (2, 3, 4, 5, 6)
LATE = (0, 1, 7)


def kernel(
    u_hbm, spread_hbm, spread_t_hbm, down_hbm, down_t_hbm, along_hbm, plane_hbm, square_hbm,
    out, drift_ref,
    u, spread, spread_t, down, down_t, along, plane, square_x,
    own, prev, rest, snd, rcv, sol, back, ahead, part, parts, total_ref,
    g, gy, gz, gx, act,
    local_sem, edge_send, edge_recv, onward_send, onward_recv, far_send, far_recv, relay,
):
    me = lax.axis_index("gx")
    x, y, c = me // 16, (me // 2) % 8, me % 2
    after, before = (me + 1) % NX, (me + NX - 1) % NX

    def device(dx, dy, core):
        return ((x + dx) % 4) * 16 + ((y + dy) % 8) * 2 + core

    barrier = pltpu.get_barrier_semaphore()

    def signal(sem, peer):
        pl.semaphore_signal(sem, inc=1, device_id={"gx": peer}, device_id_type=MESH)

    loads = [
        pltpu.make_async_copy(u_hbm.at[pl.ds(18 * d, 18)], u.at[pl.ds(18 * d, 18)], local_sem.at[d])
        for d in range(3)
    ]
    for i, (source, target) in enumerate(
        (
            (spread_hbm, spread), (down_hbm, down), (plane_hbm.at[me], plane), (square_hbm, square_x),
            (along_hbm, along), (down_t_hbm, down_t), (spread_t_hbm, spread_t),
        )
    ):
        loads.append(pltpu.make_async_copy(source, target, local_sem.at[3 + i]))
    edge_left = jnp.logical_and(y == 0, c == 0)
    edge_right = jnp.logical_and(y == 7, c == 1)
    @pl.when(edge_left)
    def _():
        signal(barrier, before)

    @pl.when(edge_right)
    def _():
        signal(barrier, after)

    signal(barrier, device(0, 0, 1 - c))
    for core in range(2):
        for dx, dy in ((0, 1), (0, 7), (1, 0), (3, 0)):
            signal(barrier, device(dx, dy, core))

    loads[0].start()
    for load in loads[1:]:
        load.start()

    def project(d, into):
        for j in range(3):
            fields = projected(
                lambda p, a, b: u[18 * d + 9 * p + 3 * a + b, pl.ds(j, ROWS, stride=3), :]
            )
            for f in range(8):
                into[pl.ds(ROWS * f, ROWS), pl.ds(128 * j, 128)] = fields[f]

    def entered():
        pl.semaphore_wait(barrier, 9 + jnp.where(jnp.logical_or(edge_left, edge_right), 1, 0))

    loads[0].wait()
    project(0, own)
    entered()
    edges = [
        pltpu.make_async_remote_copy(
            src_ref=own.at[pl.ds(96 * q, 96)], dst_ref=prev.at[pl.ds(96 * q, 96)],
            send_sem=edge_send.at[q], recv_sem=edge_recv.at[q],
            device_id={"gx": after}, device_id_type=MESH,
        )
        for q in range(2)
    ]
    for edge in edges:
        edge.start()
    for dx in (1, 3):
        signal(relay.at[0], device(dx, 0, c))
    pl.semaphore_wait(relay.at[0], 2)
    for dy in (1, 7):
        signal(relay.at[1], device(0, dy, c))
    pl.semaphore_wait(relay.at[1], 2)
    for dx in (0, 1, 3):
        for dy in (2, 6):
            signal(relay.at[2], device(dx, dy, c))

    loads[1].wait()
    project(1, act)
    middle = act[...]
    rest[...] = from_y_before(middle) - middle - own[...]
    loads[2].wait()
    project(2, act)
    middle = act[...]
    rest[...] += from_z_before(middle) - middle
    for load in loads[3:]:
        load.wait()

    factor = PEAK_SQUARE * STEP_SIZE * 0.5 / (NX * CELLS)
    filters = []
    for i in range(9):
        square = square_x[...] + plane[pl.ds(i, 1), :]
        positive = square > 0.0
        filters.append(jnp.where(positive, factor / jnp.where(positive, square, 1.0), 0.0))
    filters = jnp.concatenate(filters, axis=1)

    def place(core, chip):
        return pl.ds(36 * core + 9 * (chip // 8), 9), chip % 8

    def there(peer, core):
        return pltpu.make_async_remote_copy(
            src_ref=snd.at[place(core, peer // 2)], dst_ref=rcv.at[:, me],
            send_sem=far_send.at[0], recv_sem=far_recv.at[0],
            device_id={"gx": peer}, device_id_type=MESH,
        )

    def arrived(ref, sem):
        pltpu.make_async_copy(ref, ref, sem).wait()

    partial = None
    for q in range(2):
        edges[q].wait_recv()
        rows = pl.ds(96 * q, 96)
        fields = rest[rows, :] + prev[rows, :]
        tail = fields[48:] if q == 0 else fields
        total = 2.0 * jnp.sum(tail * tail, axis=0, keepdims=True)
        if q == 0:
            f0, f1 = fields[:24], fields[24:48]
            both = f0 + f1
            total += jnp.sum(f0 * f0 + f1 * f1 + both * both, axis=0, keepdims=True)
        partial = total if partial is None else partial + total
        forward_modes(fields, spread, down, snd, q)
        if q == 0:
            pl.semaphore_wait(relay.at[2], 6)
        for dx, dy in chips():
            there(device(dx, dy, q), q).start()

        @pl.when(c != q)
        def _():
            there(device(0, 0, q), q).start()

        @pl.when(c == q)
        def _():
            pltpu.make_async_copy(snd.at[place(q, me // 2)], rcv.at[:, me], far_recv.at[0]).start()

    partial = partial[:, :128] + partial[:, 128:256] + partial[:, 256:]
    part[0] = jnp.broadcast_to(partial, (8, 128))

    def share(stage, row, peers):
        for peer in peers:
            pltpu.make_async_remote_copy(
                src_ref=part.at[stage], dst_ref=parts.at[stage, row],
                send_sem=far_send.at[2 + stage], recv_sem=far_recv.at[2 if stage == 0 else 6],
                device_id={"gx": peer}, device_id_type=MESH,
            ).start()
        pltpu.make_async_copy(
            part.at[stage], parts.at[stage, row], far_recv.at[2 if stage == 0 else 6]
        ).start()

    share(0, y, [device(0, dy, c) for dy in range(1, 8)])


    arrived(rcv, far_recv.at[0])
    waves = times_data(along, jnp.concatenate([rcv[i] for i in range(9)], axis=1))
    waves = times_data(along, waves * filters)
    for i in range(9):
        sol[i] = waves[:, 128 * i : 128 * i + 128]

    tiles, line = place(c, me // 2)
    def came(dy):
        return jnp.where(c == 0, 1, 3 + (dy in LATE))

    for dx, dy in chips() + [(0, 0)]:
        for core in range(2):
            peer = device(dx, dy, core if dx or dy else 1 - c)
            if not (dx or dy) and core:
                continue
            pltpu.make_async_remote_copy(
                src_ref=sol.at[:, peer], dst_ref=back.at[tiles, line],
                send_sem=far_send.at[1], recv_sem=far_recv.at[came(dy)],
                device_id={"gx": peer}, device_id_type=MESH,
            ).start()
    pltpu.make_async_copy(sol.at[:, me], back.at[tiles, line], far_recv.at[came(0)]).start()

    arrived(parts.at[0], far_recv.at[2])
    part[1] = jnp.broadcast_to(jnp.sum(parts[0, :, 0, :], axis=0, keepdims=True), (8, 128))
    share(1, 2 * x + c, [device(dx, 0, core) for dx in range(1, 4) for core in range(2)] + [device(0, 0, 1 - c)])
    arrived(rcv.at[:, pl.ds(0, NX - 1)], far_send.at[0])
    arrived(parts.at[0, pl.ds(0, 7)], far_send.at[2])
    for edge in edges:
        edge.wait_send()

    def onward(rows, sem):
        pltpu.make_async_remote_copy(
            src_ref=back.at[rows], dst_ref=ahead.at[rows],
            send_sem=onward_send.at[0], recv_sem=onward_recv.at[sem],
            device_id={"gx": before}, device_id_type=MESH,
        ).start()

    first, second = pl.ds(0, 36), pl.ds(36, 36)

    def inverse(tiles, q):
        act[pl.ds(96 * q, 96), :] = inverse_fields(tiles, spread_t, down_t, (q,))

    arrived(back.at[first], far_recv.at[1])
    onward(first, 0)
    inverse(back, 0)
    for sem, group in ((3, EARLY), (4, LATE)):
        arrived(snd.at[pl.ds(0, 36), pl.ds(0, len(group))], far_recv.at[sem])
        for dy in group:
            onward((second, (y + dy) % 8), 1)
    inverse(back, 1)

    def chunks(action):
        def body(k, carry):
            i, t = k // 3, k % 3
            r, j = pl.multiple_of(8 * i, 8), pl.multiple_of(128 * t, 128)
            action(
                lambda ref, count: [ref[pl.ds(ROWS * e + r, 8), pl.ds(j, 128)] for e in range(count)],
                lambda ref, e: (ROWS * e + r, j),
                pl.ds(24 * i + t, 8, stride=3),
            )
            return carry

        lax.fori_loop(0, 9, body, 0)

    def rotate(into):
        def action(read, at, sites):
            entries = cayley(read(act, 8))
            for e in range(18):
                r, j = at(into, e)
                into[pl.ds(r, 8), pl.ds(j, 128)] = entries[e]

        chunks(action)

    rotate(g)
    whole = g[...]
    gy[...] = from_y_after(whole)
    gz[...] = from_z_after(whole)

    def update(read, at, sites):
        left = read(g, 18)
        for d, aheads in ((1, gy), (2, gz)):
            links = [u[18 * d + e, sites, :] for e in range(18)]
            new = product_dagger(product(left, links), read(aheads, 18))
            for e in range(18):
                out[18 * d + e, sites, :] = new[e]
        new = product(left, [u[e, sites, :] for e in range(18)])
        for e in range(18):
            r, j = at(gx, e)
            gx[pl.ds(r, 8), pl.ds(j, 128)] = new[e]

    chunks(update)

    arrived(parts.at[1], far_recv.at[6])
    total_ref[0] = jnp.sum(parts[1, :, 0, :]) * (1.0 / (9.0 * NX * CELLS))
    drift = pltpu.make_async_copy(total_ref, drift_ref, local_sem.at[0])
    drift.start()

    for q in range(2):
        arrived(ahead.at[first], onward_recv.at[q])
        inverse(ahead, q)

    def finish(read, at, sites):
        new = product_dagger(read(gx, 18), cayley(read(act, 8)))
        for e in range(18):
            out[e, sites, :] = new[e]

    chunks(finish)
    arrived(rcv.at[:, pl.ds(0, NX - 1)], far_send.at[1])
    arrived(parts.at[0, pl.ds(0, 7)], far_send.at[3])
    drift.wait()
    arrived(back, onward_send.at[0])


def local(gauge_links):
    tables = [jnp.asarray(t) for t in make_tables()]
    hbm = pl.BlockSpec(memory_space=pltpu.HBM)
    dma = pltpu.SemaphoreType.DMA
    fields = pltpu.VMEM((8 * ROWS, LANES), F32)
    matrix = pltpu.VMEM((18 * ROWS, LANES), F32)
    tiles = pltpu.VMEM((72, 8, 128), F32)
    waves = pltpu.VMEM((9, NX, 128), F32)
    links, drift = pl.pallas_call(
        kernel,
        out_shape=(
            pltpu.VMEM((54, 72, 128), F32),
            jax.ShapeDtypeStruct((1,), F32),
        ),
        in_specs=[hbm] * 8,
        out_specs=(pl.BlockSpec(memory_space=pltpu.VMEM), pl.BlockSpec(memory_space=pl.ANY)),
        scratch_shapes=[
            pltpu.VMEM((54, 72, 128), F32),
            pltpu.VMEM((2, LANES, 512), BF16),
            pltpu.VMEM((2, 512, LANES), BF16),
            pltpu.VMEM((2 * SIDE, SIDE), BF16),
            pltpu.VMEM((2 * SIDE, SIDE), BF16),
            pltpu.VMEM((2 * NX, NX), BF16),
            pltpu.VMEM((9, 128), F32),
            pltpu.VMEM((NX, 128), F32),
            fields, fields, fields,
            tiles, waves, waves, tiles, tiles,
            pltpu.VMEM((2, 8, 128), F32),
            pltpu.VMEM((2, 8, 8, 128), F32),
            pltpu.SMEM((1,), F32),
            matrix, matrix, matrix, matrix,
            fields,
            dma((10,)), dma((2,)), dma((2,)), dma((1,)), dma((3,)), dma((4,)), dma((7,)),
            pltpu.SemaphoreType.REGULAR((3,)),
        ],
        compiler_params=pltpu.CompilerParams(
            collective_id=0, has_side_effects=True, vmem_limit_bytes=24 << 20
        ),
    )(*[pltpu.with_memory_space_constraint(t, pltpu.HBM) for t in (gauge_links.reshape(54, 72, 128), *tables)])
    return links.reshape(gauge_links.shape), drift


def solution(mesh):
    split_x = ("ta", "gx")
    return jax.shard_map(
        local,
        mesh=mesh,
        in_specs=(P(None, None, None, None, split_x, None),),
        out_specs=(P(None, None, None, None, split_x, None), P("ta")),
        check_vma=False,
    )
```
